256 devices in a mesh: gx: 32 (over x, z_hi, core), gy: 8 (over y, z_lo).
Axes of the slice: x: 4, y: 4, z: 8 (z_hi: 4, z_lo: 2; z = z_hi * 2 + z_lo), core: 2. Of those that a mesh axis runs over, the one named last changes fastest.
Arguments:
- positions: float32 [3, 32, 16, 12, 128], P(None, 'gx', 'gy'), may hold values from 0 to 1
- velocities: float32 [3, 32, 16, 12, 128], P(None, 'gx', 'gy'), may hold values from -8 to 8
- counts: int32 [32, 16, 12], P('gx', 'gy'), may hold values from 64 to 128
Outputs:
- positions_out: float32 [3, 32, 16, 12, 128], P(None, 'gx', 'gy')
- velocities_out: float32 [3, 32, 16, 12, 128], P(None, 'gx', 'gy')
- forces_out: float32 [3, 32, 16, 12, 128], P(None, 'gx', 'gy')
The draws below stay inside these ranges and needn't reach their ends.
Inputs may be any that keep to these rules, and one draw needn't show every extreme that they name: `counts`: the number of atoms in a cell; slots from that number up to 128 are empty.
All inputs are finite; a program needn't handle non-finite values.
Results may differ from the reference program's by a relative error of at most 0.0001.
Values sent between devices are 32-bit elements; how exact they have to be, the bound alone decides.
No kernel may reach another device: no remote copies, remote signals or barrier semaphores. Data moves between devices by JAX's collectives and lax.ppermute only.
A program may use at most 64 MiB of HBM per device.

```python
import jax
import jax.numpy as jnp
from jax import lax

SLOTS = 128
NCZ = 12
STEPS = 2
NCX = 32
NCY = 16


def plant(values, stream_key, smallest, high):
    dims = values.shape
    spot = [jax.random.randint(jax.random.fold_in(stream_key, axis), (), 0, dims[axis]) for axis in range(len(dims))]
    values = values.at[tuple(spot)].set(smallest)
    longest = dims.index(max(dims))
    spot[longest] = (spot[longest] + 1) % dims[longest]
    return values.at[tuple(spot)].set(high)


def level_of(own_key, extent, pieces, least, high):
    factor_of, own = 1.0, jax.random.fold_in(own_key, 6)
    for position, blocks in pieces:
        draws = jnp.exp(jax.random.uniform(jax.random.fold_in(own, position), (blocks,), jnp.float32, least / len(pieces), high / len(pieces)))
        factor_of = factor_of * jnp.repeat(draws, extent[position] // blocks).reshape([-1 if axis == position else 1 for axis in range(len(extent))])
    return factor_of


def setup_inputs(seed: int = 0) -> dict:
    key_of = jax.random.split(jax.random.key(seed), 4)
    return {
        "positions": jnp.clip(1.0 * jax.random.uniform(key_of[0], (3, NCX, NCY, NCZ, SLOTS), jnp.float32) ** level_of(key_of[0], (3, NCX, NCY, NCZ, SLOTS), ((1, 32), (2, 8)), -0.2, 0.2), 0.0, 1.0),
        "velocities": jnp.clip(jax.random.uniform(key_of[1], (3, NCX, NCY, NCZ, SLOTS), jnp.float32, -8.0, 8.0) * level_of(key_of[1], (3, NCX, NCY, NCZ, SLOTS), ((1, 32), (2, 8)), -0.4, 0.0), -8.0, 8.0),
        "counts": plant(jax.random.randint(key_of[2], (NCX, NCY, NCZ), SLOTS // 2, SLOTS + 1), jax.random.fold_in(key_of[2], 1), SLOTS // 2, SLOTS).astype(jnp.int32),
    }


TIME_STEP = 0.05
DENSITY_SCALE = 0.0625
PAIR_SCALE = 0.0625

def neighbour_block(extended, offset_id):
    start = (jnp.int32(0), offset_id // 9, offset_id // 3 % 3, offset_id % 3, jnp.int32(0))
    target = (extended.shape[0], extended.shape[1] - 2, extended.shape[2] - 2, extended.shape[3] - 2, extended.shape[4])
    return lax.dynamic_slice(extended, start, target)

def separation(center, neighbours, offset_id):
    shifts = (offset_id // 9 - 1, offset_id // 3 % 3 - 1, offset_id % 3 - 1)
    parts = []
    for component in range(3):
        moved = neighbours[component] + shifts[component].astype(center.dtype)
        parts.append(moved[..., None, :] - center[component][..., :, None])
    return parts

def pair_terms(center, extended, filled, offset_id):
    slots = center.shape[-1]
    identity = jnp.eye(slots, dtype=center.dtype)
    neighbours = neighbour_block(extended, offset_id)
    present = neighbour_block(filled, offset_id)[0]
    parts = separation(center, neighbours, offset_id)
    square = parts[0] * parts[0] + parts[1] * parts[1] + parts[2] * parts[2]
    reach = jnp.maximum(1.0 - square, 0.0)
    selfish = (offset_id == 13).astype(center.dtype) * identity
    weights_mask = present[..., None, :] * (1.0 - selfish)
    return (parts, reach, weights_mask)

def density_pass(center, extended, filled):

    def offset_step(offset_id, running):
        offset_id = offset_id.astype(jnp.int32)
        parts, reach, weights_mask = pair_terms(center, extended, filled, offset_id)
        return running + lax.optimization_barrier(jnp.sum(weights_mask * reach * reach, axis=-1))
    start_value = jnp.zeros(center.shape[1:], center.dtype)
    return DENSITY_SCALE * lax.fori_loop(0, 27, offset_step, start_value)

def force_pass(center, present_own, slope_own, extended, filled, slope_ext):

    def offset_step(offset_id, running):
        offset_id = offset_id.astype(jnp.int32)
        parts, reach, weights_mask = pair_terms(center, extended, filled, offset_id)
        slope_near = neighbour_block(slope_ext, offset_id)[0]
        both = slope_own[..., :, None] + slope_near[..., None, :]
        coupling = weights_mask * reach * (-2.0 * DENSITY_SCALE * both - 4.0 * PAIR_SCALE * reach * reach)
        return running + 2.0 * jnp.stack([lax.optimization_barrier(jnp.sum(coupling * parts[component], axis=-1)) for component in range(3)])
    start_value = jnp.zeros(center.shape, center.dtype)
    return lax.fori_loop(0, 27, offset_step, start_value) * present_own[None]

def slots_filled(amount, slots):
    places = lax.broadcasted_iota(amount.dtype, amount.shape + (slots,), amount.ndim)
    return (places < amount[..., None]).astype(amount.dtype)

def wrap_all(field):
    return jnp.pad(field, ((0, 0), (1, 1), (1, 1), (1, 1), (0, 0)), mode='wrap')

def forces_of(positions, amount):
    slots = positions.shape[-1]
    filled_own = slots_filled(amount, slots)
    extended = wrap_all(positions)
    filled = wrap_all(filled_own[None])

    def row_density(row_index):
        center = lax.dynamic_slice_in_dim(positions, row_index, 1, 1)
        near = lax.dynamic_slice_in_dim(extended, row_index, 3, 1)
        near_filled = lax.dynamic_slice_in_dim(filled, row_index, 3, 1)
        return density_pass(center, near, near_filled)[0]
    rows = jnp.arange(NCX, dtype=jnp.int32)
    density = lax.map(row_density, rows)
    slope = -0.5 / jnp.sqrt(1.0 + density)
    slope_ext = wrap_all(slope[None])

    def row_force(row_index):
        center = lax.dynamic_slice_in_dim(positions, row_index, 1, 1)
        near = lax.dynamic_slice_in_dim(extended, row_index, 3, 1)
        near_filled = lax.dynamic_slice_in_dim(filled, row_index, 3, 1)
        present_own = lax.dynamic_slice_in_dim(filled_own, row_index, 1, 0)
        slope_own = lax.dynamic_slice_in_dim(slope, row_index, 1, 0)
        near_slope = lax.dynamic_slice_in_dim(slope_ext, row_index, 3, 1)
        return force_pass(center, present_own, slope_own, near, near_filled, near_slope)[:, 0]
    return jnp.moveaxis(lax.map(row_force, rows), 0, 1)

def reference(positions, velocities, counts):
    amount = counts.astype(jnp.float32)
    pushed = forces_of(positions, amount)
    for step_index in range(STEPS):
        velocities = velocities + 0.5 * TIME_STEP * pushed
        positions = positions + TIME_STEP * velocities
        pushed = forces_of(positions, amount)
        velocities = velocities + 0.5 * TIME_STEP * pushed
    return (positions, velocities, pushed)
```

```python
import functools

import jax
import jax.numpy as jnp
from jax import lax
from jax.experimental import pallas as pl
from jax.experimental.pallas import tpu as pltpu
from jax.sharding import PartitionSpec as P

STEPS = 2
TIME_STEP = 0.05
DENSITY_SCALE = 0.0625
FAR = 1000.0

NZ = 12
SLOTS = 128
KF = 48
COLUMNS = 12
FIRST = (0, 3)
NEAR = 9
CHUNK = 16


def split3(value):
    high = value.astype(jnp.bfloat16).astype(jnp.float32)
    rest = value - high
    middle = rest.astype(jnp.bfloat16).astype(jnp.float32)
    return high, middle, rest - middle


def stacked(values):
    row = lax.broadcasted_iota(jnp.int32, (8, SLOTS), 0)
    result = jnp.zeros((8, SLOTS), jnp.float32)
    for k, value in enumerate(values):
        result = jnp.where(row == k, value, result)
    return result


def cell_rows(ref, p, jy, c):
    return [
        jnp.broadcast_to(ref[k, p, jy, pl.ds(c, 1), :], (8, SLOTS)) for k in range(3)
    ]


def build_features(ext_ref, slope_ref, near_bf, exact, own_bf):
    def per_cell(c, carry):
        for jy in range(4):
            for p in range(3):
                x, y, z = cell_rows(ext_ref, p, jy, c)
                x, y, z = x + (p - 1.5), y + float(jy - 1), z - 0.5
                norm = 1.0 - (x * x + y * y + z * z)
                high, middle, low = split3(stacked([x, y, z, norm, 1.0]))
                features = jnp.concatenate([high, high, middle, middle, high, low], axis=0)
                place = (jy * 3 + p) * SLOTS
                near_bf[c, :, place : place + SLOTS] = features.astype(jnp.bfloat16)
                if exact is not None:
                    slope = jnp.broadcast_to(0.5 * slope_ref[p, jy, pl.ds(c, 1), :], (8, SLOTS))
                    exact[c, jy * 3 + p] = stacked([x, y, z, slope])
        for iy in range(2):
            x, y, z = cell_rows(ext_ref, 1, iy + 1, c)
            x, y = x - 0.5, y + float(iy)
            for r in range(3):
                zr = z - (r - 0.5)
                norm = -(x * x + y * y + zr * zr)
                high, middle, low = split3(stacked([2.0 * x, 2.0 * y, 2.0 * zr, 1.0, norm]))
                features = jnp.concatenate([high, middle, high, middle, low, high], axis=0)
                own_bf[c, iy, r] = features.T.astype(jnp.bfloat16)
        return carry

    lax.fori_loop(0, NZ, per_cell, 0)


def slab_of(c, r):
    return lax.rem(c + (r + NZ - 1), NZ)


def density_kernel(ext_ref, slope_ref, near_bf, own_bf):
    build_features(ext_ref, None, near_bf, None, own_bf)

    def per_cell(c, carry):
        for iy in range(2):
            total = jnp.zeros((SLOTS, SLOTS), jnp.float32)
            for r in range(3):
                slab = slab_of(c, r)
                own = own_bf[c, iy, r]
                for at in range(0, NEAR, 2):
                    width = min(2, NEAR - at)
                    place = (FIRST[iy] + at) * SLOTS
                    near = near_bf[slab, :, place : place + width * SLOTS]
                    reach = jnp.maximum(
                        jnp.dot(own, near, preferred_element_type=jnp.float32), 0.0
                    )
                    square = reach * reach
                    for k in range(width):
                        total = total + square[:, k * SLOTS : (k + 1) * SLOTS]
            density = DENSITY_SCALE * (jnp.sum(total.T, axis=0, keepdims=True) - 1.0)
            slope_ref[iy, pl.ds(c, 1), :] = -0.5 * lax.rsqrt(1.0 + jnp.maximum(density, 0.0))
        return carry

    lax.fori_loop(0, NZ, per_cell, 0)


def force_kernel(
    ext_ref, slope_ref, force_ref, near_bf, exact, own_bf, reach_a, reach_b, sums
):
    build_features(ext_ref, slope_ref, near_bf, exact, own_bf)
    reaches = (reach_a, reach_b)

    def reach_of(c, iy, r, at, width):
        place = (FIRST[iy] + at) * SLOTS
        near = near_bf[slab_of(c, r), :, place : place + width * SLOTS]
        place = (r * NEAR + at) * SLOTS
        reaches[iy][:, place : place + width * SLOTS] = jnp.maximum(
            jnp.dot(own_bf[c, iy, r], near, preferred_element_type=jnp.float32), 0.0
        )

    tiles = [(r, at, min(2, NEAR - at)) for r in range(3) for at in range(0, NEAR, 2)]
    for tile in tiles:
        reach_of(0, 0, *tile)

    def per_cell(c, carry):
        for iy in range(2):
            ahead = [(c, 1)] if iy == 0 else [(lax.rem(c + 1, NZ), 0)]
            slope_own = jnp.broadcast_to(
                0.5 * slope_ref[1, iy + 1, pl.ds(c, 1), :], (SLOTS, SLOTS)
            ).T
            step = 0
            pending = list(tiles)
            for start in range(0, SLOTS, CHUNK):
                shape = (CHUNK, SLOTS)
                total = [jnp.zeros(shape, jnp.float32) for _ in range(4)]
                slope_i = slope_own[start : start + CHUNK]
                for r in range(3):
                    slab = slab_of(c, r)
                    weight = jnp.zeros(shape, jnp.float32)
                    for at in range(NEAR):
                        if step % 14 == 0 and pending:
                            reach_of(*ahead[0], *pending.pop(0))
                        step += 1
                        x, y, z, slope = (
                            jnp.broadcast_to(exact[slab, FIRST[iy] + at, k : k + 1, :], shape)
                            for k in range(4)
                        )
                        place = (r * NEAR + at) * SLOTS
                        w = reaches[iy][start : start + CHUNK, place : place + SLOTS]
                        coupling = w * ((w * w + slope) + slope_i)
                        weight = weight + coupling
                        total[0] = total[0] + coupling * x
                        total[1] = total[1] + coupling * y
                        total[2] = total[2] + coupling * z
                    total[3] = total[3] + weight
                    if r != 1:
                        total[2] = total[2] + float(r - 1) * weight
                for k in range(4):
                    sums[k, start : start + CHUNK, :] = total[k]
            assert not pending
            folded = [jnp.sum(sums[k].T, axis=0, keepdims=True) for k in range(4)]
            own = (
                ext_ref[0, 1, iy + 1, pl.ds(c, 1), :] - 0.5,
                ext_ref[1, 1, iy + 1, pl.ds(c, 1), :] + float(iy),
                ext_ref[2, 1, iy + 1, pl.ds(c, 1), :] - 0.5,
            )
            for k in range(3):
                force_ref[k, iy, pl.ds(c, 1), :] = -0.5 * (folded[k] - own[k] * folded[3])
        return carry

    lax.fori_loop(0, NZ, per_cell, 0)


VMEM = pl.BlockSpec(memory_space=pltpu.VMEM)
FEATURES = [
    pltpu.VMEM((NZ, KF, COLUMNS * SLOTS), jnp.bfloat16),
    pltpu.VMEM((NZ, 2, 3, SLOTS, KF), jnp.bfloat16),
]


def density_call(ext):
    return pl.pallas_call(
        density_kernel,
        out_shape=jax.ShapeDtypeStruct((2, NZ, SLOTS), jnp.float32),
        in_specs=[VMEM],
        out_specs=VMEM,
        scratch_shapes=FEATURES,
        compiler_params=pltpu.CompilerParams(vmem_limit_bytes=40 * 2**20),
        cost_estimate=pl.CostEstimate(flops=10**9, bytes_accessed=10**6, transcendentals=0),
    )(ext)


def force_call(ext, slope_ext):
    reach = pltpu.VMEM((SLOTS, 3 * NEAR * SLOTS), jnp.float32)
    return pl.pallas_call(
        force_kernel,
        out_shape=jax.ShapeDtypeStruct((3, 2, NZ, SLOTS), jnp.float32),
        in_specs=[VMEM, VMEM],
        out_specs=VMEM,
        scratch_shapes=[
            FEATURES[0],
            pltpu.VMEM((NZ, COLUMNS, 8, SLOTS), jnp.float32),
            FEATURES[1],
            reach,
            reach,
            pltpu.VMEM((4, SLOTS, SLOTS), jnp.float32),
        ],
        compiler_params=pltpu.CompilerParams(vmem_limit_bytes=40 * 2**20),
        cost_estimate=pl.CostEstimate(flops=10**9, bytes_accessed=10**6, transcendentals=0),
    )(ext, slope_ext)


def swap(value, axis, odd):
    n = lax.axis_size(axis)
    partner = [(i + 1 if i % 2 == odd else i - 1) % n for i in range(n)]
    return lax.ppermute(value, axis, [(i, partner[i]) for i in range(n)])


def with_halo(value):
    even = lax.axis_index("gy") % 2 == 0
    first, last = value[..., :1, :, :], value[..., 1:, :, :]
    near = swap(jnp.where(even, last, first), "gy", 0)
    far = swap(jnp.where(even, first, last), "gy", 1)
    below, above = jnp.where(even, far, near), jnp.where(even, near, far)
    row = jnp.concatenate([below, value, above], axis=-3)
    even = lax.axis_index("gx") % 2 == 0
    near = swap(row, "gx", 0)
    far = swap(row, "gx", 1)
    before, after = jnp.where(even, far, near), jnp.where(even, near, far)
    return jnp.stack([before, row, after], axis=-4)


def shards(positions, velocities, counts):
    positions, velocities = positions[:, 0], velocities[:, 0]
    places = lax.broadcasted_iota(jnp.int32, (2, NZ, SLOTS), 2)
    present = (places < counts[0][..., None])[None]

    def forces_of(positions):
        ext = with_halo(jnp.where(present, positions, FAR))
        slope = density_call(ext)
        return jnp.where(present, force_call(ext, with_halo(slope)), 0.0)

    pushed = forces_of(positions)
    for _ in range(STEPS):
        velocities = velocities + 0.5 * TIME_STEP * pushed
        positions = positions + TIME_STEP * velocities
        pushed = forces_of(positions)
        velocities = velocities + 0.5 * TIME_STEP * pushed
    return (positions[:, None], velocities[:, None], pushed[:, None])


def solution(mesh):
    in_specs = (
        P(None, "gx", "gy", None, None),
        P(None, "gx", "gy", None, None),
        P("gx", "gy", None),
    )
    out_specs = (P(None, "gx", "gy", None, None),) * 3
    return jax.shard_map(shards, mesh=mesh, in_specs=in_specs, out_specs=out_specs, check_vma=False)
```

```python
import functools

import jax
import jax.numpy as jnp
from jax import lax
from jax.experimental import pallas as pl
from jax.experimental.pallas import tpu as pltpu
from jax.sharding import PartitionSpec as P

STEPS = 2
TIME_STEP = 0.05
DENSITY_SCALE = 0.0625
FAR = 1000.0

NZ = 12
SLOTS = 128
KF = 48
CHUNK = 16
UNROLL = 2
INNER = ((0, 4), (0, 4))
MIDDLE = ((0, 2), (0, 2))
OUTER = ((0, 3), (3, 6))


def split3(value):
    high = value.astype(jnp.bfloat16).astype(jnp.float32)
    rest = value - high
    middle = rest.astype(jnp.bfloat16).astype(jnp.float32)
    return high, middle, rest - middle


def stacked(values):
    row = lax.broadcasted_iota(jnp.int32, (8, SLOTS), 0)
    result = jnp.zeros((8, SLOTS), jnp.float32)
    for k, value in enumerate(values):
        result = jnp.where(row == k, value, result)
    return result


def rows_of(ref, column, c):
    return [
        jnp.broadcast_to(ref[k, column, pl.ds(c, 1), :], (8, SLOTS)) for k in range(3)
    ]


def build_near(near_ref, near_bf):
    def per_cell(c, carry):
        for column in range(near_ref.shape[1]):
            x, y, z = rows_of(near_ref, column, c)
            norm = 1.0 - (x * x + y * y + z * z)
            high, middle, low = split3(stacked([x, y, z, norm, 1.0]))
            features = jnp.concatenate([high, high, middle, middle, high, low], axis=0)
            place = column * SLOTS
            near_bf[c, :, place : place + SLOTS] = features.astype(jnp.bfloat16)
        return carry

    lax.fori_loop(0, NZ, per_cell, 0, unroll=2)


def build_own(own_ref, own_bf):
    def per_cell(c, carry):
        for iy in range(2):
            x, y, z = rows_of(own_ref, iy, c)
            for r in range(3):
                zr = z - float(r - 1)
                norm = -(x * x + y * y + zr * zr)
                high, middle, low = split3(stacked([2.0 * x, 2.0 * y, 2.0 * zr, 1.0, norm]))
                features = jnp.concatenate([high, middle, high, middle, low, high], axis=0)
                own_bf[c, iy, r] = features.T.astype(jnp.bfloat16)
        return carry

    lax.fori_loop(0, NZ, per_cell, 0, unroll=2)


def slab_of(c, r):
    return lax.rem(c + (r + NZ - 1), NZ)


def density_kernel(spans, fresh, own_ref, near_ref, sum_ref, near_bf, *refs):
    if fresh:
        own_bf, totals_a, totals_b = refs
        build_own(own_ref, own_bf)
    else:
        own_bf = own_ref
        totals_a, totals_b = refs
    build_near(near_ref, near_bf)
    totals = (totals_a, totals_b)

    def fold(c, iy):
        sum_ref[iy, pl.ds(c, 1), :] = jnp.sum(totals[iy][...].T, axis=0, keepdims=True)

    def per_cell(c, carry):
        for iy in range(2):
            if iy == 0:
                fold(jnp.maximum(c - 1, 0), 1)
            else:
                fold(c, 0)
            first, last = spans[iy]
            total = jnp.zeros((SLOTS, SLOTS), jnp.float32)
            for r in range(3):
                slab = slab_of(c, r)
                own = own_bf[c, iy, r]
                for at in range(first, last, 2):
                    width = min(2, last - at)
                    near = near_bf[slab, :, at * SLOTS : (at + width) * SLOTS]
                    reach = jnp.maximum(
                        jnp.dot(own, near, preferred_element_type=jnp.float32), 0.0
                    )
                    square = reach * reach
                    for k in range(width):
                        total = total + square[:, k * SLOTS : (k + 1) * SLOTS]
            totals[iy][...] = total
        return carry

    totals_b[...] = jnp.zeros((SLOTS, SLOTS), jnp.float32)
    lax.fori_loop(0, NZ, per_cell, 0, unroll=UNROLL)
    fold(NZ - 1, 1)


def force_kernel(spans, fresh, own_ref, near_ref, own_bf, near_bf, own_slope_ref, *refs):
    if fresh:
        near_slope_ref, force_ref, slope_own, reach_a, reach_b, sums_a, sums_b = refs

        def turn(c, carry):
            for iy in range(2):
                slope_own[c, iy] = jnp.broadcast_to(
                    own_slope_ref[iy, pl.ds(c, 1), :], (SLOTS, SLOTS)
                ).T
            return carry

        lax.fori_loop(0, NZ, turn, 0, unroll=3)
    else:
        slope_own = own_slope_ref
        near_slope_ref, force_ref, reach_a, reach_b, sums_a, sums_b = refs
    reaches = (reach_a, reach_b)
    sums = (sums_a, sums_b)

    def reach_of(c, iy, r, at, width):
        first, last = spans[iy]
        near = near_bf[slab_of(c, r), :, (first + at) * SLOTS : (first + at + width) * SLOTS]
        place = (r * (last - first) + at) * SLOTS
        reaches[iy][:, place : place + width * SLOTS] = jnp.maximum(
            jnp.dot(own_bf[c, iy, r], near, preferred_element_type=jnp.float32), 0.0
        )

    def fold(c, iy):
        folded = [jnp.sum(sums[iy][k].T, axis=0, keepdims=True) for k in range(4)]
        for k in range(3):
            own = own_ref[k, iy, pl.ds(c, 1), :]
            force_ref[k, iy, pl.ds(c, 1), :] = -0.5 * (folded[k] - own * folded[3])

    count = spans[0][1] - spans[0][0]
    tiles = [(r, at, min(2, count - at)) for r in range(3) for at in range(0, count, 2)]
    for tile in tiles:
        reach_of(0, 0, *tile)
    steps = (SLOTS // CHUNK) * 3 * count
    every = max(1, (steps * 3 // 4) // len(tiles))

    def per_cell(c, carry):
        for iy in range(2):
            if iy == 0:
                fold(jnp.maximum(c - 1, 0), 1)
            else:
                fold(c, 0)
            ahead = (c, 1) if iy == 0 else (lax.rem(c + 1, NZ), 0)
            step = 0
            pending = list(tiles)
            first, last = spans[iy]
            for start in range(0, SLOTS, CHUNK):
                shape = (CHUNK, SLOTS)
                total = [jnp.zeros(shape, jnp.float32) for _ in range(4)]
                slope_i = slope_own[c, iy, start : start + CHUNK, :]
                for r in range(3):
                    slab = slab_of(c, r)
                    weight = jnp.zeros(shape, jnp.float32)
                    for at in range(first, last):
                        if step % every == 0 and pending:
                            reach_of(*ahead, *pending.pop(0))
                        step += 1
                        x, y, z = (
                            jnp.broadcast_to(near_ref[k, at, pl.ds(slab, 1), :], shape)
                            for k in range(3)
                        )
                        slope = jnp.broadcast_to(near_slope_ref[at, pl.ds(slab, 1), :], shape)
                        place = (r * count + at - first) * SLOTS
                        w = reaches[iy][start : start + CHUNK, place : place + SLOTS]
                        coupling = w * ((w * w + slope) + slope_i)
                        weight = weight + coupling
                        total[0] = total[0] + coupling * x
                        total[1] = total[1] + coupling * y
                        total[2] = total[2] + coupling * z
                    total[3] = total[3] + weight
                    if r != 1:
                        total[2] = total[2] + float(r - 1) * weight
                for k in range(4):
                    sums[iy][k, start : start + CHUNK, :] = total[k]
            assert not pending
        return carry

    sums_b[...] = jnp.zeros((4, SLOTS, SLOTS), jnp.float32)
    lax.fori_loop(0, NZ, per_cell, 0)
    fold(NZ - 1, 1)


VMEM = pl.BlockSpec(memory_space=pltpu.VMEM)
SQUARE = pltpu.VMEM((SLOTS, SLOTS), jnp.float32)
OWN_FEATURES = jax.ShapeDtypeStruct((NZ, 2, 3, SLOTS, KF), jnp.bfloat16)
OWN_SLOPES = jax.ShapeDtypeStruct((NZ, 2, SLOTS, SLOTS), jnp.float32)


def call(kernel, out_shape, scratch, *operands):
    return pl.pallas_call(
        kernel,
        out_shape=out_shape,
        in_specs=[VMEM] * len(operands),
        out_specs=jax.tree.map(lambda _: VMEM, out_shape),
        scratch_shapes=scratch,
        compiler_params=pltpu.CompilerParams(vmem_limit_bytes=32 * 2**20),
        cost_estimate=pl.CostEstimate(flops=10**9, bytes_accessed=10**6, transcendentals=0),
    )(*operands)


def density_part(own, near, spans):
    fresh = own.dtype == jnp.float32
    out_shape = [
        jax.ShapeDtypeStruct((2, NZ, SLOTS), jnp.float32),
        jax.ShapeDtypeStruct((NZ, KF, near.shape[1] * SLOTS), jnp.bfloat16),
    ]
    if fresh:
        out_shape.append(OWN_FEATURES)
    kernel = functools.partial(density_kernel, spans, fresh)
    return call(kernel, out_shape, [SQUARE, SQUARE], own, near)


def force_part(own, near, own_bf, near_bf, own_slope, near_slope, spans):
    fresh = own_slope.ndim == 3
    out_shape = [jax.ShapeDtypeStruct((3, 2, NZ, SLOTS), jnp.float32)]
    if fresh:
        out_shape.append(OWN_SLOPES)
    count = spans[0][1] - spans[0][0]
    reach = pltpu.VMEM((SLOTS, 3 * count * SLOTS), jnp.float32)
    sums = pltpu.VMEM((4, SLOTS, SLOTS), jnp.float32)
    kernel = functools.partial(force_kernel, spans, fresh)
    return call(
        kernel,
        out_shape,
        [reach, reach, sums, sums],
        own,
        near,
        own_bf,
        near_bf,
        own_slope,
        near_slope,
    )


def swap(value, axis, odd):
    n = lax.axis_size(axis)
    partner = [(i + 1 if i % 2 == odd else i - 1) % n for i in range(n)]
    return lax.ppermute(value, axis, [(i, partner[i]) for i in range(n)])


def along(component, amount):
    unit = [0.0, 0.0, 0.0]
    unit[component] = 1.0
    return jnp.array(unit, jnp.float32).reshape(3, 1, 1, 1) * amount


def exchange_x(value):
    return swap(value, "gx", 0), swap(value, "gx", 1)


def exchange_y(value):
    even = lax.axis_index("gy") % 2 == 0
    first, last = value
    near = swap(jnp.where(even, last, first), "gy", 0)
    far = swap(jnp.where(even, first, last), "gy", 1)
    return near, far


def below_above(received):
    even = lax.axis_index("gy") % 2 == 0
    near, far = received
    return jnp.where(even, far, near), jnp.where(even, near, far)


def rows_along_y(*blocks):
    return [jnp.stack([block[..., iy, :, :] for block in blocks], axis=-3) for iy in range(2)]


def shards(positions, velocities, counts):
    positions, velocities = positions[:, 0], velocities[:, 0]
    places = lax.broadcasted_iota(jnp.int32, (2, NZ, SLOTS), 2)
    present = (places < counts[0][..., None])[None]
    frame = jnp.stack(
        [
            jnp.full((2, 1, 1), -0.5, jnp.float32),
            jnp.array([-1.0, 0.0], jnp.float32).reshape(2, 1, 1),
            jnp.full((2, 1, 1), -0.5, jnp.float32),
        ]
    )
    side = jnp.where(lax.axis_index("gx") % 2 == 0, 1.0, -1.0)

    def forces_of(positions):
        own = jnp.where(present, positions + frame, FAR)
        near, far = exchange_x(own)
        near = near + along(0, side)
        inner = jnp.concatenate([own, near], axis=1)
        square, inner_bf, own_bf = density_part(own, inner, INNER)
        square, far = lax.optimization_barrier((square, far))
        far = far - along(0, side)
        received = exchange_y(rows_along_y(own, near, far))
        part, far_bf = density_part(own_bf, far, MIDDLE)
        part, received = lax.optimization_barrier((part, received))
        below, above = below_above(received)
        outer = jnp.concatenate([below - along(1, 2.0), above + along(1, 2.0)], axis=1)
        last, outer_bf = density_part(own_bf, outer, OUTER)
        density = DENSITY_SCALE * jnp.maximum(square + part + last - 1.0, 0.0)
        slope = -0.25 * lax.rsqrt(1.0 + density)
        near_slope, far_slope = exchange_x(slope)
        inner_slope = jnp.concatenate([slope, near_slope], axis=0)
        force, turned = force_part(own, inner, own_bf, inner_bf, slope, inner_slope, INNER)
        force, far_slope = lax.optimization_barrier((force, far_slope))
        received = exchange_y(rows_along_y(slope, near_slope, far_slope))
        (part,) = force_part(own, far, own_bf, far_bf, turned, far_slope, MIDDLE)
        part, received = lax.optimization_barrier((part, received))
        outer_slope = jnp.concatenate(below_above(received), axis=0)
        (last,) = force_part(own, outer, own_bf, outer_bf, turned, outer_slope, OUTER)
        force = force + part + last
        return jnp.where(present, force, 0.0)

    pushed = forces_of(positions)
    for _ in range(STEPS):
        velocities = velocities + 0.5 * TIME_STEP * pushed
        positions = positions + TIME_STEP * velocities
        pushed = forces_of(positions)
        velocities = velocities + 0.5 * TIME_STEP * pushed
    return (positions[:, None], velocities[:, None], pushed[:, None])


def solution(mesh):
    in_specs = (
        P(None, "gx", "gy", None, None),
        P(None, "gx", "gy", None, None),
        P("gx", "gy", None),
    )
    out_specs = (P(None, "gx", "gy", None, None),) * 3
    return jax.shard_map(shards, mesh=mesh, in_specs=in_specs, out_specs=out_specs, check_vma=False)
```

```python
import functools

import jax
import jax.numpy as jnp
from jax import lax
from jax.experimental import pallas as pl
from jax.experimental.pallas import tpu as pltpu
from jax.sharding import PartitionSpec as P

STEPS = 2
TIME_STEP = 0.05
DENSITY_SCALE = 0.0625
FAR = 1000.0

NZ = 12
SLOTS = 128
KF = 48
CHUNK = 16
UNROLL = 4
INNER = ((0, 3), (0, 3))
MIDDLE = ((0, 3), (0, 3))
OUTER = ((0, 3), (3, 6))


def split3(value):
    high = value.astype(jnp.bfloat16).astype(jnp.float32)
    rest = value - high
    middle = rest.astype(jnp.bfloat16).astype(jnp.float32)
    return high, middle, rest - middle


def stacked(values):
    row = lax.broadcasted_iota(jnp.int32, (8, SLOTS), 0)
    result = jnp.zeros((8, SLOTS), jnp.float32)
    for k, value in enumerate(values):
        result = jnp.where(row == k, value, result)
    return result


def rows_of(ref, column, c):
    return [
        jnp.broadcast_to(ref[k, column, pl.ds(c, 1), :], (8, SLOTS)) for k in range(3)
    ]


def build_near(near_ref, near_bf):
    def per_cell(c, carry):
        for column in range(near_ref.shape[1]):
            x, y, z = rows_of(near_ref, column, c)
            norm = 1.0 - (x * x + y * y + z * z)
            high, middle, low = split3(stacked([x, y, z, norm, 1.0]))
            features = jnp.concatenate([high, high, middle, middle, high, low], axis=0)
            place = column * SLOTS
            near_bf[c, :, place : place + SLOTS] = features.astype(jnp.bfloat16)
        return carry

    lax.fori_loop(0, NZ, per_cell, 0, unroll=2)


def build_own(own_ref, own_bf):
    def per_cell(c, carry):
        for iy in range(2):
            x, y, z = rows_of(own_ref, iy, c)
            for r in range(3):
                zr = z - float(r - 1)
                norm = -(x * x + y * y + zr * zr)
                high, middle, low = split3(stacked([2.0 * x, 2.0 * y, 2.0 * zr, 1.0, norm]))
                features = jnp.concatenate([high, middle, high, middle, low, high], axis=0)
                own_bf[c, iy, r] = features.T.astype(jnp.bfloat16)
        return carry

    lax.fori_loop(0, NZ, per_cell, 0, unroll=2)


def slab_of(c, r):
    if isinstance(c, int):
        return (c + r + NZ - 1) % NZ
    if r == 1:
        return c
    return jnp.where(c == 0, NZ - 1, c - 1) if r == 0 else jnp.where(c == NZ - 1, 0, c + 1)


def density_kernel(spans, fresh, own_ref, near_ref, sum_ref, near_bf, *refs):
    if fresh:
        own_bf, totals_a, totals_b = refs
        build_own(own_ref, own_bf)
    else:
        own_bf = own_ref
        totals_a, totals_b = refs
    build_near(near_ref, near_bf)
    totals = (totals_a, totals_b)

    def fold(c, iy):
        sum_ref[iy, pl.ds(c, 1), :] = jnp.sum(totals[iy][...].T, axis=0, keepdims=True)

    def per_cell(c, carry):
        for iy in range(2):
            if iy == 0:
                fold(jnp.maximum(c - 1, 0), 1)
            else:
                fold(c, 0)
            first, last = spans[iy]
            total = jnp.zeros((SLOTS, SLOTS), jnp.float32)
            for r in range(3):
                slab = slab_of(c, r)
                own = own_bf[c, iy, r]
                for at in range(first, last, 2):
                    width = min(2, last - at)
                    near = near_bf[slab, :, at * SLOTS : (at + width) * SLOTS]
                    reach = jnp.maximum(
                        jnp.dot(own, near, preferred_element_type=jnp.float32), 0.0
                    )
                    square = reach * reach
                    for k in range(width):
                        total = total + square[:, k * SLOTS : (k + 1) * SLOTS]
            totals[iy][...] = total
        return carry

    totals_b[...] = jnp.zeros((SLOTS, SLOTS), jnp.float32)
    lax.fori_loop(0, NZ, per_cell, 0, unroll=UNROLL)
    fold(NZ - 1, 1)


def force_kernel(spans, fresh, own_ref, near_ref, own_bf, near_bf, own_slope_ref, *refs):
    if fresh:
        near_slope_ref, force_ref, slope_own, reach_a, reach_b, sums_a, sums_b = refs

        def turn(c, carry):
            for iy in range(2):
                slope_own[c, iy] = jnp.broadcast_to(
                    own_slope_ref[iy, pl.ds(c, 1), :], (SLOTS, SLOTS)
                ).T
            return carry

        lax.fori_loop(0, NZ, turn, 0, unroll=3)
    else:
        slope_own = own_slope_ref
        near_slope_ref, force_ref, reach_a, reach_b, sums_a, sums_b = refs
    reaches = (reach_a, reach_b)
    sums = (sums_a, sums_b)

    def reach_of(c, iy, r, at, width):
        first, last = spans[iy]
        near = near_bf[slab_of(c, r), :, (first + at) * SLOTS : (first + at + width) * SLOTS]
        place = (r * (last - first) + at) * SLOTS
        reaches[iy][:, place : place + width * SLOTS] = jnp.maximum(
            jnp.dot(own_bf[c, iy, r], near, preferred_element_type=jnp.float32), 0.0
        )

    def fold(c, iy):
        folded = [jnp.sum(sums[iy][k].T, axis=0, keepdims=True) for k in range(4)]
        for k in range(3):
            own = own_ref[k, iy, pl.ds(c, 1), :]
            force_ref[k, iy, pl.ds(c, 1), :] = -0.5 * (folded[k] - own * folded[3])

    count = spans[0][1] - spans[0][0]
    tiles = [(r, at, min(2, count - at)) for r in range(3) for at in range(0, count, 2)]
    for tile in tiles:
        reach_of(0, 0, *tile)
    steps = (SLOTS // CHUNK) * 3 * count
    every = max(1, (steps * 3 // 4) // len(tiles))

    def per_cell(c, carry):
        for iy in range(2):
            if iy == 0:
                fold(jnp.maximum(c - 1, 0), 1)
            else:
                fold(c, 0)
            ahead = (c, 1) if iy == 0 else (slab_of(c, 2), 0)
            step = 0
            pending = list(tiles)
            first, last = spans[iy]
            for start in range(0, SLOTS, CHUNK):
                shape = (CHUNK, SLOTS)
                total = [jnp.zeros(shape, jnp.float32) for _ in range(4)]
                slope_i = slope_own[c, iy, start : start + CHUNK, :]
                for r in range(3):
                    slab = slab_of(c, r)
                    weight = jnp.zeros(shape, jnp.float32)
                    for at in range(first, last):
                        if step % every == 0 and pending:
                            reach_of(*ahead, *pending.pop(0))
                        step += 1
                        x, y, z = (
                            jnp.broadcast_to(near_ref[k, at, pl.ds(slab, 1), :], shape)
                            for k in range(3)
                        )
                        slope = jnp.broadcast_to(near_slope_ref[at, pl.ds(slab, 1), :], shape)
                        place = (r * count + at - first) * SLOTS
                        w = reaches[iy][start : start + CHUNK, place : place + SLOTS]
                        coupling = w * ((w * w + slope) + slope_i)
                        weight = weight + coupling
                        total[0] = total[0] + coupling * x
                        total[1] = total[1] + coupling * y
                        total[2] = total[2] + coupling * z
                    total[3] = total[3] + weight
                    if r != 1:
                        total[2] = total[2] + float(r - 1) * weight
                for k in range(4):
                    sums[iy][k, start : start + CHUNK, :] = total[k]
            assert not pending
        return carry

    sums_b[...] = jnp.zeros((4, SLOTS, SLOTS), jnp.float32)
    lax.fori_loop(0, NZ, per_cell, 0)
    fold(NZ - 1, 1)


VMEM = pl.BlockSpec(memory_space=pltpu.VMEM)
SQUARE = pltpu.VMEM((SLOTS, SLOTS), jnp.float32)
OWN_FEATURES = jax.ShapeDtypeStruct((NZ, 2, 3, SLOTS, KF), jnp.bfloat16)
OWN_SLOPES = jax.ShapeDtypeStruct((NZ, 2, SLOTS, SLOTS), jnp.float32)


def call(kernel, out_shape, scratch, *operands):
    return pl.pallas_call(
        kernel,
        out_shape=out_shape,
        in_specs=[VMEM] * len(operands),
        out_specs=jax.tree.map(lambda _: VMEM, out_shape),
        scratch_shapes=scratch,
        compiler_params=pltpu.CompilerParams(vmem_limit_bytes=32 * 2**20),
        cost_estimate=pl.CostEstimate(flops=10**9, bytes_accessed=10**6, transcendentals=0),
    )(*operands)


def density_part(own, near, spans):
    fresh = own.dtype == jnp.float32
    out_shape = [
        jax.ShapeDtypeStruct((2, NZ, SLOTS), jnp.float32),
        jax.ShapeDtypeStruct((NZ, KF, near.shape[1] * SLOTS), jnp.bfloat16),
    ]
    if fresh:
        out_shape.append(OWN_FEATURES)
    kernel = functools.partial(density_kernel, spans, fresh)
    return call(kernel, out_shape, [SQUARE, SQUARE], own, near)


def force_part(own, near, own_bf, near_bf, own_slope, near_slope, spans):
    fresh = own_slope.ndim == 3
    out_shape = [jax.ShapeDtypeStruct((3, 2, NZ, SLOTS), jnp.float32)]
    if fresh:
        out_shape.append(OWN_SLOPES)
    count = spans[0][1] - spans[0][0]
    reach = pltpu.VMEM((SLOTS, 3 * count * SLOTS), jnp.float32)
    sums = pltpu.VMEM((4, SLOTS, SLOTS), jnp.float32)
    kernel = functools.partial(force_kernel, spans, fresh)
    return call(
        kernel,
        out_shape,
        [reach, reach, sums, sums],
        own,
        near,
        own_bf,
        near_bf,
        own_slope,
        near_slope,
    )


def finish_kernel(counts_ref, position_ref, velocity_ref, *refs):
    *parts, position_out, velocity_out, force_out = refs
    lane = lax.broadcasted_iota(jnp.int32, (NZ, SLOTS), 1)
    for iy in range(2):
        present = lane < counts_ref[iy]
        for k in range(3):
            force = jnp.where(present, sum(part[k, iy] for part in parts), 0.0)
            force_out[k, :, iy, :] = force
            velocity_out[k, :, iy, :] = velocity_ref[k, iy] + 0.5 * TIME_STEP * force
            position_out[k, :, iy, :] = position_ref[k, iy]


def finish(positions, velocities, counts, parts):
    counts = jnp.broadcast_to(counts[..., None], (2, NZ, SLOTS))
    outs = pl.pallas_call(
        finish_kernel,
        out_shape=[jax.ShapeDtypeStruct((3, NZ, 2, SLOTS), jnp.float32)] * 3,
        in_specs=[VMEM] * (3 + len(parts)),
        compiler_params=pltpu.CompilerParams(vmem_limit_bytes=8 * 2**20),
    )(counts, positions, velocities, *parts)
    return tuple(out.transpose(0, 2, 1, 3)[:, None] for out in outs)


def swap(value, axis, odd):
    n = lax.axis_size(axis)
    partner = [(i + 1 if i % 2 == odd else i - 1) % n for i in range(n)]
    return lax.ppermute(value, axis, [(i, partner[i]) for i in range(n)])


def along(component, amount):
    unit = [0.0, 0.0, 0.0]
    unit[component] = 1.0
    return jnp.array(unit, jnp.float32).reshape(3, 1, 1, 1) * amount


def exchange_x(value):
    return swap(value, "gx", 0), swap(value, "gx", 1)


def exchange_y(value):
    even = lax.axis_index("gy") % 2 == 0
    first, last = value
    near = swap(jnp.where(even, last, first), "gy", 0)
    far = swap(jnp.where(even, first, last), "gy", 1)
    return near, far


def below_above(received):
    even = lax.axis_index("gy") % 2 == 0
    near, far = received
    return jnp.where(even, far, near), jnp.where(even, near, far)


def rows_along_y(*blocks):
    return [jnp.stack([block[..., iy, :, :] for block in blocks], axis=-3) for iy in range(2)]


def shards(positions, velocities, counts):
    positions, velocities = positions[:, 0], velocities[:, 0]
    places = lax.broadcasted_iota(jnp.int32, (2, NZ, SLOTS), 2)
    present = (places < counts[0][..., None])[None]
    frame = jnp.stack(
        [
            jnp.full((2, 1, 1), -0.5, jnp.float32),
            jnp.array([-1.0, 0.0], jnp.float32).reshape(2, 1, 1),
            jnp.full((2, 1, 1), -0.5, jnp.float32),
        ]
    )
    side = jnp.where(lax.axis_index("gx") % 2 == 0, 1.0, -1.0)

    def forces_of(positions):
        own = jnp.where(present, positions + frame, FAR)
        near, far = exchange_x(own)
        near = near + along(0, side)
        inner = jnp.concatenate([own, near[:, :1]], axis=1)
        square, inner_bf, own_bf = density_part(own, inner, INNER)
        square, far = lax.optimization_barrier((square, far))
        far = far - along(0, side)
        received = exchange_y(rows_along_y(own, near, far))
        middle = jnp.concatenate([near[:, 1:], far], axis=1)
        part, middle_bf = density_part(own_bf, middle, MIDDLE)
        part, received = lax.optimization_barrier((part, received))
        below, above = below_above(received)
        outer = jnp.concatenate([below - along(1, 2.0), above + along(1, 2.0)], axis=1)
        last, outer_bf = density_part(own_bf, outer, OUTER)
        density = DENSITY_SCALE * jnp.maximum(square + part + last - 1.0, 0.0)
        slope = -0.25 * lax.rsqrt(1.0 + density)
        near_slope, far_slope = exchange_x(slope)
        inner_slope = jnp.concatenate([slope, near_slope[:1]], axis=0)
        force, turned = force_part(own, inner, own_bf, inner_bf, slope, inner_slope, INNER)
        force, far_slope = lax.optimization_barrier((force, far_slope))
        received = exchange_y(rows_along_y(slope, near_slope, far_slope))
        middle_slope = jnp.concatenate([near_slope[1:], far_slope], axis=0)
        (part,) = force_part(own, middle, own_bf, middle_bf, turned, middle_slope, MIDDLE)
        part, received = lax.optimization_barrier((part, received))
        outer_slope = jnp.concatenate(below_above(received), axis=0)
        (last,) = force_part(own, outer, own_bf, outer_bf, turned, outer_slope, OUTER)
        return force, part, last

    parts = forces_of(positions)
    for step in range(STEPS):
        if step:
            pushed = jnp.where(present, sum(parts), 0.0)
            velocities = velocities + 0.5 * TIME_STEP * pushed
        else:
            pushed = jnp.where(present, sum(parts), 0.0)
        velocities = velocities + 0.5 * TIME_STEP * pushed
        positions = positions + TIME_STEP * velocities
        parts = forces_of(positions)
    return finish(positions, velocities, counts[0], parts)


def solution(mesh):
    in_specs = (
        P(None, "gx", "gy", None, None),
        P(None, "gx", "gy", None, None),
        P("gx", "gy", None),
    )
    out_specs = (P(None, "gx", "gy", None, None),) * 3
    return jax.shard_map(shards, mesh=mesh, in_specs=in_specs, out_specs=out_specs, check_vma=False)
```

```python
import functools

import jax
import jax.numpy as jnp
from jax import lax
from jax.experimental import pallas as pl
from jax.experimental.pallas import tpu as pltpu
from jax.sharding import PartitionSpec as P

STEPS = 2
TIME_STEP = 0.05
DENSITY_SCALE = 0.0625
FAR = 1000.0

NZ = 12
SLOTS = 128
KF = 48
CHUNK = 16
UNROLL = 4
INNER = ((0, 3), (0, 3))
MIDDLE = ((0, 3), (0, 3))
OUTER = ((0, 3), (3, 6))


def split3(value):
    high = value.astype(jnp.bfloat16).astype(jnp.float32)
    rest = value - high
    middle = rest.astype(jnp.bfloat16).astype(jnp.float32)
    return high, middle, rest - middle


def stacked(values):
    row = lax.broadcasted_iota(jnp.int32, (8, SLOTS), 0)
    result = jnp.zeros((8, SLOTS), jnp.float32)
    for k, value in enumerate(values):
        result = jnp.where(row == k, value, result)
    return result


def rows_of(ref, column, c):
    return [
        jnp.broadcast_to(ref[k, column, pl.ds(c, 1), :], (8, SLOTS)) for k in range(3)
    ]


def build_near(near_ref, near_bf):
    def per_cell(c, carry):
        for column in range(near_ref.shape[1]):
            x, y, z = rows_of(near_ref, column, c)
            norm = 1.0 - (x * x + y * y + z * z)
            high, middle, low = split3(stacked([x, y, z, norm, 1.0]))
            features = jnp.concatenate([high, high, middle, middle, high, low], axis=0)
            place = column * SLOTS
            near_bf[c, :, place : place + SLOTS] = features.astype(jnp.bfloat16)
        return carry

    lax.fori_loop(0, NZ, per_cell, 0, unroll=2)


def build_own(own_ref, own_bf):
    def per_cell(c, carry):
        for iy in range(2):
            x, y, z = rows_of(own_ref, iy, c)
            for r in range(3):
                zr = z - float(r - 1)
                norm = -(x * x + y * y + zr * zr)
                high, middle, low = split3(stacked([2.0 * x, 2.0 * y, 2.0 * zr, 1.0, norm]))
                features = jnp.concatenate([high, middle, high, middle, low, high], axis=0)
                own_bf[c, iy, r] = features.T.astype(jnp.bfloat16)
        return carry

    lax.fori_loop(0, NZ, per_cell, 0, unroll=4)


def slab_of(c, r):
    if isinstance(c, int):
        return (c + r + NZ - 1) % NZ
    if r == 1:
        return c
    return jnp.where(c == 0, NZ - 1, c - 1) if r == 0 else jnp.where(c == NZ - 1, 0, c + 1)


def density_kernel(spans, fresh, own_ref, near_ref, sum_ref, near_bf, *refs):
    if fresh:
        own_bf, totals_a, totals_b = refs
        build_own(own_ref, own_bf)
    else:
        own_bf = own_ref
        totals_a, totals_b = refs
    build_near(near_ref, near_bf)
    totals = (totals_a, totals_b)

    def fold(c, iy):
        sum_ref[iy, pl.ds(c, 1), :] = jnp.sum(totals[iy][...].T, axis=0, keepdims=True)

    def per_cell(c, carry):
        for iy in range(2):
            if iy == 0:
                fold(jnp.maximum(c - 1, 0), 1)
            else:
                fold(c, 0)
            first, last = spans[iy]
            total = jnp.zeros((SLOTS, SLOTS), jnp.float32)
            for r in range(3):
                slab = slab_of(c, r)
                own = own_bf[c, iy, r]
                for at in range(first, last, 2):
                    width = min(2, last - at)
                    near = near_bf[slab, :, at * SLOTS : (at + width) * SLOTS]
                    reach = jnp.maximum(
                        jnp.dot(own, near, preferred_element_type=jnp.float32), 0.0
                    )
                    square = reach * reach
                    for k in range(width):
                        total = total + square[:, k * SLOTS : (k + 1) * SLOTS]
            totals[iy][...] = total
        return carry

    totals_b[...] = jnp.zeros((SLOTS, SLOTS), jnp.float32)
    lax.fori_loop(0, NZ, per_cell, 0, unroll=UNROLL)
    fold(NZ - 1, 1)


def force_kernel(spans, fresh, own_ref, near_ref, own_bf, near_bf, own_slope_ref, *refs):
    if fresh:
        near_slope_ref, force_ref, slope_own, reach_a, reach_b, sums_a, sums_b = refs

        def turn(c, carry):
            for iy in range(2):
                slope_own[c, iy] = jnp.broadcast_to(
                    own_slope_ref[iy, pl.ds(c, 1), :], (SLOTS, SLOTS)
                ).T
            return carry

        lax.fori_loop(0, NZ, turn, 0, unroll=3)
    else:
        slope_own = own_slope_ref
        near_slope_ref, force_ref, reach_a, reach_b, sums_a, sums_b = refs
    reaches = (reach_a, reach_b)
    sums = (sums_a, sums_b)

    def reach_of(c, iy, r, at, width):
        first, last = spans[iy]
        near = near_bf[slab_of(c, r), :, (first + at) * SLOTS : (first + at + width) * SLOTS]
        place = (r * (last - first) + at) * SLOTS
        reaches[iy][:, place : place + width * SLOTS] = jnp.maximum(
            jnp.dot(own_bf[c, iy, r], near, preferred_element_type=jnp.float32), 0.0
        )

    def fold(c, iy):
        folded = [jnp.sum(sums[iy][k].T, axis=0, keepdims=True) for k in range(4)]
        for k in range(3):
            own = own_ref[k, iy, pl.ds(c, 1), :]
            force_ref[k, iy, pl.ds(c, 1), :] = -0.5 * (folded[k] - own * folded[3])

    count = spans[0][1] - spans[0][0]
    tiles = [(r, at, min(2, count - at)) for r in range(3) for at in range(0, count, 2)]
    for tile in tiles:
        reach_of(0, 0, *tile)
    steps = (SLOTS // CHUNK) * 3 * count
    every = max(1, (steps * 3 // 4) // len(tiles))

    def per_cell(c, carry):
        for iy in range(2):
            if iy == 0:
                fold(jnp.maximum(c - 1, 0), 1)
            else:
                fold(c, 0)
            ahead = (c, 1) if iy == 0 else (slab_of(c, 2), 0)
            step = 0
            pending = list(tiles)
            first, last = spans[iy]
            for start in range(0, SLOTS, CHUNK):
                shape = (CHUNK, SLOTS)
                total = [jnp.zeros(shape, jnp.float32) for _ in range(4)]
                slope_i = slope_own[c, iy, start : start + CHUNK, :]
                for r in range(3):
                    slab = slab_of(c, r)
                    weight = jnp.zeros(shape, jnp.float32)
                    for at in range(first, last):
                        if step % every == 0 and pending:
                            reach_of(*ahead, *pending.pop(0))
                        step += 1
                        x, y, z = (
                            jnp.broadcast_to(near_ref[k, at, pl.ds(slab, 1), :], shape)
                            for k in range(3)
                        )
                        slope = jnp.broadcast_to(near_slope_ref[at, pl.ds(slab, 1), :], shape)
                        place = (r * count + at - first) * SLOTS
                        w = reaches[iy][start : start + CHUNK, place : place + SLOTS]
                        coupling = w * ((w * w + slope) + slope_i)
                        weight = weight + coupling
                        total[0] = total[0] + coupling * x
                        total[1] = total[1] + coupling * y
                        total[2] = total[2] + coupling * z
                    total[3] = total[3] + weight
                    if r != 1:
                        total[2] = total[2] + float(r - 1) * weight
                for k in range(4):
                    sums[iy][k, start : start + CHUNK, :] = total[k]
            assert not pending
        return carry

    sums_b[...] = jnp.zeros((4, SLOTS, SLOTS), jnp.float32)
    lax.fori_loop(0, NZ, per_cell, 0, unroll=2)
    fold(NZ - 1, 1)


VMEM = pl.BlockSpec(memory_space=pltpu.VMEM)
SQUARE = pltpu.VMEM((SLOTS, SLOTS), jnp.float32)
OWN_FEATURES = jax.ShapeDtypeStruct((NZ, 2, 3, SLOTS, KF), jnp.bfloat16)
OWN_SLOPES = jax.ShapeDtypeStruct((NZ, 2, SLOTS, SLOTS), jnp.float32)


def call(kernel, out_shape, scratch, *operands):
    return pl.pallas_call(
        kernel,
        out_shape=out_shape,
        in_specs=[VMEM] * len(operands),
        out_specs=jax.tree.map(lambda _: VMEM, out_shape),
        scratch_shapes=scratch,
        compiler_params=pltpu.CompilerParams(vmem_limit_bytes=32 * 2**20),
        cost_estimate=pl.CostEstimate(flops=10**9, bytes_accessed=10**6, transcendentals=0),
    )(*operands)


def density_part(own, near, spans):
    fresh = own.dtype == jnp.float32
    out_shape = [
        jax.ShapeDtypeStruct((2, NZ, SLOTS), jnp.float32),
        jax.ShapeDtypeStruct((NZ, KF, near.shape[1] * SLOTS), jnp.bfloat16),
    ]
    if fresh:
        out_shape.append(OWN_FEATURES)
    kernel = functools.partial(density_kernel, spans, fresh)
    return call(kernel, out_shape, [SQUARE, SQUARE], own, near)


def force_part(own, near, own_bf, near_bf, own_slope, near_slope, spans):
    fresh = own_slope.ndim == 3
    out_shape = [jax.ShapeDtypeStruct((3, 2, NZ, SLOTS), jnp.float32)]
    if fresh:
        out_shape.append(OWN_SLOPES)
    count = spans[0][1] - spans[0][0]
    reach = pltpu.VMEM((SLOTS, 3 * count * SLOTS), jnp.float32)
    sums = pltpu.VMEM((4, SLOTS, SLOTS), jnp.float32)
    kernel = functools.partial(force_kernel, spans, fresh)
    return call(
        kernel,
        out_shape,
        [reach, reach, sums, sums],
        own,
        near,
        own_bf,
        near_bf,
        own_slope,
        near_slope,
    )


def finish_kernel(mark_ref, position_ref, velocity_ref, *refs):
    *parts, position_out, velocity_out, force_out = refs
    for iy in range(2):
        present = mark_ref[iy] < 0.5 * FAR
        for k in range(3):
            force = jnp.where(present, sum(part[k, iy] for part in parts), 0.0)
            force_out[k, :, iy, :] = force
            velocity_out[k, :, iy, :] = velocity_ref[k, iy] + 0.5 * TIME_STEP * force
            position_out[k, :, iy, :] = position_ref[k, iy]


def finish(positions, velocities, mark, parts):
    outs = pl.pallas_call(
        finish_kernel,
        out_shape=[jax.ShapeDtypeStruct((3, NZ, 2, SLOTS), jnp.float32)] * 3,
        in_specs=[VMEM] * (3 + len(parts)),
        compiler_params=pltpu.CompilerParams(vmem_limit_bytes=8 * 2**20),
    )(mark, positions, velocities, *parts)
    return tuple(out.transpose(0, 2, 1, 3)[:, None] for out in outs)


def swap(value, axis, odd):
    n = lax.axis_size(axis)
    partner = [(i + 1 if i % 2 == odd else i - 1) % n for i in range(n)]
    return lax.ppermute(value, axis, [(i, partner[i]) for i in range(n)])


def along(component, amount):
    unit = [0.0, 0.0, 0.0]
    unit[component] = 1.0
    return jnp.array(unit, jnp.float32).reshape(3, 1, 1, 1) * amount


def exchange_x(value):
    return swap(value, "gx", 0), swap(value, "gx", 1)


def exchange_y(value):
    even = lax.axis_index("gy") % 2 == 0
    first, last = value
    far = swap(jnp.where(even, first, last), "gy", 1)
    near = swap(jnp.where(even, last, first), "gy", 0)
    return near, far


def below_above(received):
    even = lax.axis_index("gy") % 2 == 0
    near, far = received
    return jnp.where(even, far, near), jnp.where(even, near, far)


def rows_along_y(*blocks):
    return [jnp.stack([block[..., iy, :, :] for block in blocks], axis=-3) for iy in range(2)]


def shards(positions, velocities, counts):
    positions, velocities = positions[:, 0], velocities[:, 0]
    places = lax.broadcasted_iota(jnp.int32, (2, NZ, SLOTS), 2)
    frame = jnp.stack(
        [
            jnp.full((2, 1, 1), -0.5, jnp.float32),
            jnp.array([-1.0, 0.0], jnp.float32).reshape(2, 1, 1),
            jnp.full((2, 1, 1), -0.5, jnp.float32),
        ]
    )
    side = jnp.where(lax.axis_index("gx") % 2 == 0, 1.0, -1.0)

    def forces_of(own):
        near, far = exchange_x(own)
        near = near + along(0, side)
        inner = jnp.concatenate([own, near[:, :1]], axis=1)
        square, inner_bf, own_bf = density_part(own, inner, INNER)
        square, far = lax.optimization_barrier((square, far))
        far = far - along(0, side)
        received = exchange_y(rows_along_y(own, near, far))
        middle = jnp.concatenate([near[:, 1:], far], axis=1)
        part, middle_bf = density_part(own_bf, middle, MIDDLE)
        part, received = lax.optimization_barrier((part, received))
        below, above = below_above(received)
        outer = jnp.concatenate([below - along(1, 2.0), above + along(1, 2.0)], axis=1)
        last, outer_bf = density_part(own_bf, outer, OUTER)
        density = DENSITY_SCALE * jnp.maximum(square + part + last - 1.0, 0.0)
        slope = -0.25 * lax.rsqrt(1.0 + density)
        near_slope, far_slope = exchange_x(slope)
        inner_slope = jnp.concatenate([slope, near_slope[:1]], axis=0)
        force, turned = force_part(own, inner, own_bf, inner_bf, slope, inner_slope, INNER)
        force, far_slope = lax.optimization_barrier((force, far_slope))
        received = exchange_y(rows_along_y(slope, near_slope, far_slope))
        middle_slope = jnp.concatenate([near_slope[1:], far_slope], axis=0)
        (part,) = force_part(own, middle, own_bf, middle_bf, turned, middle_slope, MIDDLE)
        part, received = lax.optimization_barrier((part, received))
        outer_slope = jnp.concatenate(below_above(received), axis=0)
        (last,) = force_part(own, outer, own_bf, outer_bf, turned, outer_slope, OUTER)
        return force, part, last

    own = jnp.where((places < counts[0][..., None])[None], positions + frame, FAR)
    mark = own[0]
    present = (mark < 0.5 * FAR)[None]
    parts = forces_of(own)
    for step in range(STEPS):
        pushed = jnp.where(present, sum(parts), 0.0)
        if step:
            velocities = velocities + 0.5 * TIME_STEP * pushed
        velocities = velocities + 0.5 * TIME_STEP * pushed
        positions = positions + TIME_STEP * velocities
        parts = forces_of(jnp.where(present, positions + frame, FAR))
    return finish(positions, velocities, mark, parts)


def solution(mesh):
    in_specs = (
        P(None, "gx", "gy", None, None),
        P(None, "gx", "gy", None, None),
        P("gx", "gy", None),
    )
    out_specs = (P(None, "gx", "gy", None, None),) * 3
    return jax.shard_map(shards, mesh=mesh, in_specs=in_specs, out_specs=out_specs, check_vma=False)
```

```python
import functools

import jax
import jax.numpy as jnp
from jax import lax
from jax.experimental import pallas as pl
from jax.experimental.pallas import tpu as pltpu
from jax.sharding import PartitionSpec as P

STEPS = 2
TIME_STEP = 0.05
DENSITY_SCALE = 0.0625
FAR = 1000.0

NZ = 12
SLOTS = 128
KF = 48
CHUNK = 16
UNROLL = 4
INNER = ((0, 3), (0, 3))
MIDDLE = ((0, 3), (0, 3))
OUTER = ((0, 3), (3, 6))


def split3(value):
    high = value.astype(jnp.bfloat16).astype(jnp.float32)
    rest = value - high
    middle = rest.astype(jnp.bfloat16).astype(jnp.float32)
    return high, middle, rest - middle


def stacked(values):
    row = lax.broadcasted_iota(jnp.int32, (8, SLOTS), 0)
    result = jnp.zeros((8, SLOTS), jnp.float32)
    for k, value in enumerate(values):
        result = jnp.where(row == k, value, result)
    return result


def rows_of(ref, column, c):
    return [
        jnp.broadcast_to(ref[k, column, pl.ds(c, 1), :], (8, SLOTS)) for k in range(3)
    ]


def build_near(near_ref, near_bf):
    def per_cell(c, carry):
        for column in range(near_ref.shape[1]):
            x, y, z = rows_of(near_ref, column, c)
            norm = 1.0 - (x * x + y * y + z * z)
            high, middle, low = split3(stacked([x, y, z, norm, 1.0]))
            features = jnp.concatenate([high, high, middle, middle, high, low], axis=0)
            place = column * SLOTS
            near_bf[c, :, place : place + SLOTS] = features.astype(jnp.bfloat16)
        return carry

    lax.fori_loop(0, NZ, per_cell, 0, unroll=2)


def build_own(own_ref, own_bf):
    def per_cell(c, carry):
        for iy in range(2):
            x, y, z = rows_of(own_ref, iy, c)
            for r in range(3):
                zr = z - float(r - 1)
                norm = -(x * x + y * y + zr * zr)
                high, middle, low = split3(stacked([2.0 * x, 2.0 * y, 2.0 * zr, 1.0, norm]))
                features = jnp.concatenate([high, middle, high, middle, low, high], axis=0)
                own_bf[c, iy, r] = features.T.astype(jnp.bfloat16)
        return carry

    lax.fori_loop(0, NZ, per_cell, 0, unroll=4)


def slab_of(c, r):
    if isinstance(c, int):
        return (c + r + NZ - 1) % NZ
    if r == 1:
        return c
    return jnp.where(c == 0, NZ - 1, c - 1) if r == 0 else jnp.where(c == NZ - 1, 0, c + 1)


def density_kernel(spans, fresh, own_ref, near_ref, sum_ref, near_bf, *refs):
    if fresh:
        own_bf, totals_a, totals_b = refs
        build_own(own_ref, own_bf)
    else:
        own_bf = own_ref
        totals_a, totals_b = refs
    build_near(near_ref, near_bf)
    totals = (totals_a, totals_b)

    def fold(c, iy):
        sum_ref[iy, pl.ds(c, 1), :] = jnp.sum(totals[iy][...].T, axis=0, keepdims=True)

    def per_cell(c, carry):
        for iy in range(2):
            if iy == 0:
                fold(jnp.maximum(c - 1, 0), 1)
            else:
                fold(c, 0)
            first, last = spans[iy]
            total = jnp.zeros((SLOTS, SLOTS), jnp.float32)
            for r in range(3):
                slab = slab_of(c, r)
                own = own_bf[c, iy, r]
                for at in range(first, last, 2):
                    width = min(2, last - at)
                    near = near_bf[slab, :, at * SLOTS : (at + width) * SLOTS]
                    reach = jnp.maximum(
                        jnp.dot(own, near, preferred_element_type=jnp.float32), 0.0
                    )
                    square = reach * reach
                    for k in range(width):
                        total = total + square[:, k * SLOTS : (k + 1) * SLOTS]
            totals[iy][...] = total
        return carry

    totals_b[...] = jnp.zeros((SLOTS, SLOTS), jnp.float32)
    lax.fori_loop(0, NZ, per_cell, 0, unroll=UNROLL)
    fold(NZ - 1, 1)


def force_kernel(spans, fresh, own_ref, near_ref, own_bf, near_bf, own_slope_ref, *refs):
    if fresh:
        near_slope_ref, force_ref, slope_own, reach_a, reach_b, sums_a, sums_b = refs

        def turn(c, carry):
            for iy in range(2):
                slope_own[c, iy] = jnp.broadcast_to(
                    own_slope_ref[iy, pl.ds(c, 1), :], (SLOTS, SLOTS)
                ).T
            return carry

        lax.fori_loop(0, NZ, turn, 0, unroll=3)
    else:
        slope_own = own_slope_ref
        near_slope_ref, force_ref, reach_a, reach_b, sums_a, sums_b = refs
    reaches = (reach_a, reach_b)
    sums = (sums_a, sums_b)

    def reach_of(c, iy, r, at, width):
        first, last = spans[iy]
        near = near_bf[slab_of(c, r), :, (first + at) * SLOTS : (first + at + width) * SLOTS]
        place = (r * (last - first) + at) * SLOTS
        reaches[iy][:, place : place + width * SLOTS] = jnp.maximum(
            jnp.dot(own_bf[c, iy, r], near, preferred_element_type=jnp.float32), 0.0
        )

    def fold(c, iy):
        folded = [jnp.sum(sums[iy][k].T, axis=0, keepdims=True) for k in range(4)]
        for k in range(3):
            own = own_ref[k, iy, pl.ds(c, 1), :]
            force_ref[k, iy, pl.ds(c, 1), :] = -0.5 * (folded[k] - own * folded[3])

    count = spans[0][1] - spans[0][0]
    tiles = [(r, at, min(2, count - at)) for r in range(3) for at in range(0, count, 2)]
    for tile in tiles:
        reach_of(0, 0, *tile)
    steps = (SLOTS // CHUNK) * 3 * count
    every = max(1, (steps * 3 // 4) // len(tiles))

    def per_cell(c, carry):
        for iy in range(2):
            if iy == 0:
                fold(jnp.maximum(c - 1, 0), 1)
            else:
                fold(c, 0)
            ahead = (c, 1) if iy == 0 else (slab_of(c, 2), 0)
            step = 0
            pending = list(tiles)
            first, last = spans[iy]
            for start in range(0, SLOTS, CHUNK):
                shape = (CHUNK, SLOTS)
                total = [jnp.zeros(shape, jnp.float32) for _ in range(4)]
                slope_i = slope_own[c, iy, start : start + CHUNK, :]
                for r in range(3):
                    slab = slab_of(c, r)
                    weight = jnp.zeros(shape, jnp.float32)
                    for at in range(first, last):
                        if step % every == 0 and pending:
                            reach_of(*ahead, *pending.pop(0))
                        step += 1
                        x, y, z = (
                            jnp.broadcast_to(near_ref[k, at, pl.ds(slab, 1), :], shape)
                            for k in range(3)
                        )
                        slope = jnp.broadcast_to(near_slope_ref[at, pl.ds(slab, 1), :], shape)
                        place = (r * count + at - first) * SLOTS
                        w = reaches[iy][start : start + CHUNK, place : place + SLOTS]
                        coupling = w * ((w * w + slope) + slope_i)
                        weight = weight + coupling
                        total[0] = total[0] + coupling * x
                        total[1] = total[1] + coupling * y
                        total[2] = total[2] + coupling * z
                    total[3] = total[3] + weight
                    if r != 1:
                        total[2] = total[2] + float(r - 1) * weight
                for k in range(4):
                    sums[iy][k, start : start + CHUNK, :] = total[k]
            assert not pending
        return carry

    sums_b[...] = jnp.zeros((4, SLOTS, SLOTS), jnp.float32)
    lax.fori_loop(0, NZ, per_cell, 0, unroll=2)
    fold(NZ - 1, 1)


VMEM = pl.BlockSpec(memory_space=pltpu.VMEM)
SQUARE = pltpu.VMEM((SLOTS, SLOTS), jnp.float32)
OWN_FEATURES = jax.ShapeDtypeStruct((NZ, 2, 3, SLOTS, KF), jnp.bfloat16)
OWN_SLOPES = jax.ShapeDtypeStruct((NZ, 2, SLOTS, SLOTS), jnp.float32)


def call(kernel, out_shape, scratch, *operands):
    return pl.pallas_call(
        kernel,
        out_shape=out_shape,
        in_specs=[VMEM] * len(operands),
        out_specs=jax.tree.map(lambda _: VMEM, out_shape),
        scratch_shapes=scratch,
        compiler_params=pltpu.CompilerParams(vmem_limit_bytes=32 * 2**20),
        cost_estimate=pl.CostEstimate(flops=10**9, bytes_accessed=10**6, transcendentals=0),
    )(*operands)


def density_part(own, near, spans):
    fresh = own.dtype == jnp.float32
    out_shape = [
        jax.ShapeDtypeStruct((2, NZ, SLOTS), jnp.float32),
        jax.ShapeDtypeStruct((NZ, KF, near.shape[1] * SLOTS), jnp.bfloat16),
    ]
    if fresh:
        out_shape.append(OWN_FEATURES)
    kernel = functools.partial(density_kernel, spans, fresh)
    return call(kernel, out_shape, [SQUARE, SQUARE], own, near)


def force_part(own, near, own_bf, near_bf, own_slope, near_slope, spans):
    fresh = own_slope.ndim == 3
    out_shape = [jax.ShapeDtypeStruct((3, 2, NZ, SLOTS), jnp.float32)]
    if fresh:
        out_shape.append(OWN_SLOPES)
    count = spans[0][1] - spans[0][0]
    reach = pltpu.VMEM((SLOTS, 3 * count * SLOTS), jnp.float32)
    sums = pltpu.VMEM((4, SLOTS, SLOTS), jnp.float32)
    kernel = functools.partial(force_kernel, spans, fresh)
    return call(
        kernel,
        out_shape,
        [reach, reach, sums, sums],
        own,
        near,
        own_bf,
        near_bf,
        own_slope,
        near_slope,
    )


def finish_kernel(mark_ref, position_ref, velocity_ref, *refs):
    *parts, position_out, velocity_out, force_out = refs
    for iy in range(2):
        present = mark_ref[iy] < 0.5 * FAR
        for k in range(3):
            force = jnp.where(present, sum(part[k, iy] for part in parts), 0.0)
            force_out[k, :, iy, :] = force
            velocity_out[k, :, iy, :] = velocity_ref[k, iy] + 0.5 * TIME_STEP * force
            position_out[k, :, iy, :] = position_ref[k, iy]


def finish(positions, velocities, mark, parts):
    outs = pl.pallas_call(
        finish_kernel,
        out_shape=[jax.ShapeDtypeStruct((3, NZ, 2, SLOTS), jnp.float32)] * 3,
        in_specs=[VMEM] * (3 + len(parts)),
        compiler_params=pltpu.CompilerParams(vmem_limit_bytes=8 * 2**20),
    )(mark, positions, velocities, *parts)
    return tuple(out.transpose(0, 2, 1, 3)[:, None] for out in outs)


def swap(value, axis, odd):
    n = lax.axis_size(axis)
    partner = [(i + 1 if i % 2 == odd else i - 1) % n for i in range(n)]
    return lax.ppermute(value, axis, [(i, partner[i]) for i in range(n)])


def along(component, amount):
    unit = [0.0, 0.0, 0.0]
    unit[component] = 1.0
    return jnp.array(unit, jnp.float32).reshape(3, 1, 1, 1) * amount


def exchange_x(value):
    return swap(value, "gx", 0), swap(value, "gx", 1)


def exchange_y(value):
    even = lax.axis_index("gy") % 2 == 0
    first, last = value
    far = swap(jnp.where(even, first, last), "gy", 1)
    near = swap(jnp.where(even, last, first), "gy", 0)
    return far, near


def below_above(received):
    even = lax.axis_index("gy") % 2 == 0
    far, near = received
    return jnp.where(even, far, near), jnp.where(even, near, far)


def rows_along_y(*blocks):
    return [jnp.stack([block[..., iy, :, :] for block in blocks], axis=-3) for iy in range(2)]


def shards(positions, velocities, counts):
    positions, velocities = positions[:, 0], velocities[:, 0]
    places = lax.broadcasted_iota(jnp.int32, (2, NZ, SLOTS), 2)
    frame = jnp.stack(
        [
            jnp.full((2, 1, 1), -0.5, jnp.float32),
            jnp.array([-1.0, 0.0], jnp.float32).reshape(2, 1, 1),
            jnp.full((2, 1, 1), -0.5, jnp.float32),
        ]
    )
    side = jnp.where(lax.axis_index("gx") % 2 == 0, 1.0, -1.0)

    def forces_of(own):
        near, far = exchange_x(own)
        near = near + along(0, side)
        inner = jnp.concatenate([own, near[:, :1]], axis=1)
        square, inner_bf, own_bf = density_part(own, inner, INNER)
        square, far = lax.optimization_barrier((square, far))
        far = far - along(0, side)
        received = exchange_y(rows_along_y(own, near, far))
        middle = jnp.concatenate([near[:, 1:], far], axis=1)
        part, middle_bf = density_part(own_bf, middle, MIDDLE)
        part, received = lax.optimization_barrier((part, received))
        below, above = below_above(received)
        outer = jnp.concatenate([below - along(1, 2.0), above + along(1, 2.0)], axis=1)
        last, outer_bf = density_part(own_bf, outer, OUTER)
        density = DENSITY_SCALE * jnp.maximum(square + part + last - 1.0, 0.0)
        slope = -0.25 * lax.rsqrt(1.0 + density)
        near_slope, far_slope = exchange_x(slope)
        inner_slope = jnp.concatenate([slope, near_slope[:1]], axis=0)
        force, turned = force_part(own, inner, own_bf, inner_bf, slope, inner_slope, INNER)
        force, far_slope = lax.optimization_barrier((force, far_slope))
        received = exchange_y(rows_along_y(slope, near_slope, far_slope))
        middle_slope = jnp.concatenate([near_slope[1:], far_slope], axis=0)
        (part,) = force_part(own, middle, own_bf, middle_bf, turned, middle_slope, MIDDLE)
        part, received = lax.optimization_barrier((part, received))
        outer_slope = jnp.concatenate(below_above(received), axis=0)
        (last,) = force_part(own, outer, own_bf, outer_bf, turned, outer_slope, OUTER)
        return force, part, last

    own = jnp.where((places < counts[0][..., None])[None], positions + frame, FAR)
    mark = own[0]
    present = (mark < 0.5 * FAR)[None]
    parts = forces_of(own)
    for step in range(STEPS):
        pushed = jnp.where(present, sum(parts), 0.0)
        if step:
            velocities = velocities + 0.5 * TIME_STEP * pushed
        velocities = velocities + 0.5 * TIME_STEP * pushed
        positions = positions + TIME_STEP * velocities
        parts = forces_of(jnp.where(present, positions + frame, FAR))
    return finish(positions, velocities, mark, parts)


def solution(mesh):
    in_specs = (
        P(None, "gx", "gy", None, None),
        P(None, "gx", "gy", None, None),
        P("gx", "gy", None),
    )
    out_specs = (P(None, "gx", "gy", None, None),) * 3
    return jax.shard_map(shards, mesh=mesh, in_specs=in_specs, out_specs=out_specs, check_vma=False)
```

```python
import functools

import jax
import jax.numpy as jnp
from jax import lax
from jax.experimental import pallas as pl
from jax.experimental.pallas import tpu as pltpu
from jax.sharding import PartitionSpec as P

STEPS = 2
TIME_STEP = 0.05
DENSITY_SCALE = 0.0625
FAR = 1000.0

NZ = 12
SLOTS = 128
KF = 48
CHUNK = 16
UNROLL = 4
INNER = ((0, 2), (0, 2))
MIDDLE = ((0, 4), (0, 4))
OUTER = ((0, 3), (3, 6))


def split3(value):
    high = value.astype(jnp.bfloat16).astype(jnp.float32)
    rest = value - high
    middle = rest.astype(jnp.bfloat16).astype(jnp.float32)
    return high, middle, rest - middle


def stacked(values):
    row = lax.broadcasted_iota(jnp.int32, (8, SLOTS), 0)
    result = jnp.zeros((8, SLOTS), jnp.float32)
    for k, value in enumerate(values):
        result = jnp.where(row == k, value, result)
    return result


def rows_of(ref, column, c):
    return [
        jnp.broadcast_to(ref[k, column, pl.ds(c, 1), :], (8, SLOTS)) for k in range(3)
    ]


def build_near(near_ref, near_bf):
    def per_cell(c, carry):
        for column in range(near_ref.shape[1]):
            x, y, z = rows_of(near_ref, column, c)
            norm = 1.0 - (x * x + y * y + z * z)
            high, middle, low = split3(stacked([x, y, z, norm, 1.0]))
            features = jnp.concatenate([high, high, middle, middle, high, low], axis=0)
            place = column * SLOTS
            near_bf[c, :, place : place + SLOTS] = features.astype(jnp.bfloat16)
        return carry

    lax.fori_loop(0, NZ, per_cell, 0, unroll=2)


def build_own(own_ref, own_bf):
    def per_cell(c, carry):
        for iy in range(2):
            x, y, z = rows_of(own_ref, iy, c)
            for r in range(3):
                zr = z - float(r - 1)
                norm = -(x * x + y * y + zr * zr)
                high, middle, low = split3(stacked([2.0 * x, 2.0 * y, 2.0 * zr, 1.0, norm]))
                features = jnp.concatenate([high, middle, high, middle, low, high], axis=0)
                own_bf[c, iy, r] = features.T.astype(jnp.bfloat16)
        return carry

    lax.fori_loop(0, NZ, per_cell, 0, unroll=4)


def slab_of(c, r):
    if isinstance(c, int):
        return (c + r + NZ - 1) % NZ
    if r == 1:
        return c
    return jnp.where(c == 0, NZ - 1, c - 1) if r == 0 else jnp.where(c == NZ - 1, 0, c + 1)


def density_kernel(spans, fresh, own_ref, near_ref, sum_ref, near_bf, *refs):
    if fresh:
        own_bf, totals_a, totals_b = refs
        build_own(own_ref, own_bf)
    else:
        own_bf = own_ref
        totals_a, totals_b = refs
    build_near(near_ref, near_bf)
    totals = (totals_a, totals_b)

    def fold(c, iy):
        sum_ref[iy, pl.ds(c, 1), :] = jnp.sum(totals[iy][...].T, axis=0, keepdims=True)

    def per_cell(c, carry):
        for iy in range(2):
            if iy == 0:
                fold(jnp.maximum(c - 1, 0), 1)
            else:
                fold(c, 0)
            first, last = spans[iy]
            total = jnp.zeros((SLOTS, SLOTS), jnp.float32)
            for r in range(3):
                slab = slab_of(c, r)
                own = own_bf[c, iy, r]
                for at in range(first, last, 2):
                    width = min(2, last - at)
                    near = near_bf[slab, :, at * SLOTS : (at + width) * SLOTS]
                    reach = jnp.maximum(
                        jnp.dot(own, near, preferred_element_type=jnp.float32), 0.0
                    )
                    square = reach * reach
                    for k in range(width):
                        total = total + square[:, k * SLOTS : (k + 1) * SLOTS]
            totals[iy][...] = total
        return carry

    totals_b[...] = jnp.zeros((SLOTS, SLOTS), jnp.float32)
    lax.fori_loop(0, NZ, per_cell, 0, unroll=UNROLL)
    fold(NZ - 1, 1)


def force_kernel(spans, fresh, own_ref, near_ref, own_bf, near_bf, own_slope_ref, *refs):
    if fresh:
        near_slope_ref, force_ref, slope_own, reach_a, reach_b, sums_a, sums_b = refs

        def turn(c, carry):
            for iy in range(2):
                slope_own[c, iy] = jnp.broadcast_to(
                    own_slope_ref[iy, pl.ds(c, 1), :], (SLOTS, SLOTS)
                ).T
            return carry

        lax.fori_loop(0, NZ, turn, 0, unroll=3)
    else:
        slope_own = own_slope_ref
        near_slope_ref, force_ref, reach_a, reach_b, sums_a, sums_b = refs
    reaches = (reach_a, reach_b)
    sums = (sums_a, sums_b)

    def reach_of(c, iy, r, at, width):
        first, last = spans[iy]
        near = near_bf[slab_of(c, r), :, (first + at) * SLOTS : (first + at + width) * SLOTS]
        place = (r * (last - first) + at) * SLOTS
        reaches[iy][:, place : place + width * SLOTS] = jnp.maximum(
            jnp.dot(own_bf[c, iy, r], near, preferred_element_type=jnp.float32), 0.0
        )

    def fold(c, iy):
        folded = [jnp.sum(sums[iy][k].T, axis=0, keepdims=True) for k in range(4)]
        for k in range(3):
            own = own_ref[k, iy, pl.ds(c, 1), :]
            force_ref[k, iy, pl.ds(c, 1), :] = -0.5 * (folded[k] - own * folded[3])

    count = spans[0][1] - spans[0][0]
    tiles = [(r, at, min(2, count - at)) for r in range(3) for at in range(0, count, 2)]
    for tile in tiles:
        reach_of(0, 0, *tile)
    steps = (SLOTS // CHUNK) * 3 * count
    every = max(1, (steps * 3 // 4) // len(tiles))

    def per_cell(c, carry):
        for iy in range(2):
            if iy == 0:
                fold(jnp.maximum(c - 1, 0), 1)
            else:
                fold(c, 0)
            ahead = (c, 1) if iy == 0 else (slab_of(c, 2), 0)
            step = 0
            pending = list(tiles)
            first, last = spans[iy]
            for start in range(0, SLOTS, CHUNK):
                shape = (CHUNK, SLOTS)
                total = [jnp.zeros(shape, jnp.float32) for _ in range(4)]
                slope_i = slope_own[c, iy, start : start + CHUNK, :]
                for r in range(3):
                    slab = slab_of(c, r)
                    weight = jnp.zeros(shape, jnp.float32)
                    for at in range(first, last):
                        if step % every == 0 and pending:
                            reach_of(*ahead, *pending.pop(0))
                        step += 1
                        x, y, z = (
                            jnp.broadcast_to(near_ref[k, at, pl.ds(slab, 1), :], shape)
                            for k in range(3)
                        )
                        slope = jnp.broadcast_to(near_slope_ref[at, pl.ds(slab, 1), :], shape)
                        place = (r * count + at - first) * SLOTS
                        w = reaches[iy][start : start + CHUNK, place : place + SLOTS]
                        coupling = w * ((w * w + slope) + slope_i)
                        weight = weight + coupling
                        total[0] = total[0] + coupling * x
                        total[1] = total[1] + coupling * y
                        total[2] = total[2] + coupling * z
                    total[3] = total[3] + weight
                    if r != 1:
                        total[2] = total[2] + float(r - 1) * weight
                for k in range(4):
                    sums[iy][k, start : start + CHUNK, :] = total[k]
            assert not pending
        return carry

    sums_b[...] = jnp.zeros((4, SLOTS, SLOTS), jnp.float32)
    lax.fori_loop(0, NZ, per_cell, 0, unroll=2)
    fold(NZ - 1, 1)


VMEM = pl.BlockSpec(memory_space=pltpu.VMEM)
SQUARE = pltpu.VMEM((SLOTS, SLOTS), jnp.float32)
OWN_FEATURES = jax.ShapeDtypeStruct((NZ, 2, 3, SLOTS, KF), jnp.bfloat16)
OWN_SLOPES = jax.ShapeDtypeStruct((NZ, 2, SLOTS, SLOTS), jnp.float32)


def call(kernel, out_shape, scratch, *operands):
    return pl.pallas_call(
        kernel,
        out_shape=out_shape,
        in_specs=[VMEM] * len(operands),
        out_specs=jax.tree.map(lambda _: VMEM, out_shape),
        scratch_shapes=scratch,
        compiler_params=pltpu.CompilerParams(vmem_limit_bytes=32 * 2**20),
        cost_estimate=pl.CostEstimate(flops=10**9, bytes_accessed=10**6, transcendentals=0),
    )(*operands)


def density_part(own, near, spans):
    fresh = own.dtype == jnp.float32
    out_shape = [
        jax.ShapeDtypeStruct((2, NZ, SLOTS), jnp.float32),
        jax.ShapeDtypeStruct((NZ, KF, near.shape[1] * SLOTS), jnp.bfloat16),
    ]
    if fresh:
        out_shape.append(OWN_FEATURES)
    kernel = functools.partial(density_kernel, spans, fresh)
    return call(kernel, out_shape, [SQUARE, SQUARE], own, near)


def force_part(own, near, own_bf, near_bf, own_slope, near_slope, spans):
    fresh = own_slope.ndim == 3
    out_shape = [jax.ShapeDtypeStruct((3, 2, NZ, SLOTS), jnp.float32)]
    if fresh:
        out_shape.append(OWN_SLOPES)
    count = spans[0][1] - spans[0][0]
    reach = pltpu.VMEM((SLOTS, 3 * count * SLOTS), jnp.float32)
    sums = pltpu.VMEM((4, SLOTS, SLOTS), jnp.float32)
    kernel = functools.partial(force_kernel, spans, fresh)
    return call(
        kernel,
        out_shape,
        [reach, reach, sums, sums],
        own,
        near,
        own_bf,
        near_bf,
        own_slope,
        near_slope,
    )


def finish_kernel(mark_ref, position_ref, velocity_ref, *refs):
    *parts, position_out, velocity_out, force_out = refs
    for iy in range(2):
        present = mark_ref[iy] < 0.5 * FAR
        for k in range(3):
            force = jnp.where(present, sum(part[k, iy] for part in parts), 0.0)
            force_out[k, :, iy, :] = force
            velocity_out[k, :, iy, :] = velocity_ref[k, iy] + 0.5 * TIME_STEP * force
            position_out[k, :, iy, :] = position_ref[k, iy]


def finish(positions, velocities, mark, parts):
    outs = pl.pallas_call(
        finish_kernel,
        out_shape=[jax.ShapeDtypeStruct((3, NZ, 2, SLOTS), jnp.float32)] * 3,
        in_specs=[VMEM] * (3 + len(parts)),
        compiler_params=pltpu.CompilerParams(vmem_limit_bytes=8 * 2**20),
    )(mark, positions, velocities, *parts)
    return tuple(out.transpose(0, 2, 1, 3)[:, None] for out in outs)


def swap(value, axis, odd):
    n = lax.axis_size(axis)
    partner = [(i + 1 if i % 2 == odd else i - 1) % n for i in range(n)]
    return lax.ppermute(value, axis, [(i, partner[i]) for i in range(n)])


def along(component, amount):
    unit = [0.0, 0.0, 0.0]
    unit[component] = 1.0
    return jnp.array(unit, jnp.float32).reshape(3, 1, 1, 1) * amount


def exchange_x(value):
    far = swap(value, "gx", 1)
    return swap(value, "gx", 0), far


def exchange_y(value):
    even = lax.axis_index("gy") % 2 == 0
    first, last = value
    far = swap(jnp.where(even, first, last), "gy", 1)
    near = swap(jnp.where(even, last, first), "gy", 0)
    return far, near


def below_above(received):
    even = lax.axis_index("gy") % 2 == 0
    far, near = received
    return jnp.where(even, far, near), jnp.where(even, near, far)


def rows_along_y(*blocks):
    return [jnp.stack([block[..., iy, :, :] for block in blocks], axis=-3) for iy in range(2)]


def shards(positions, velocities, counts):
    positions, velocities = positions[:, 0], velocities[:, 0]
    places = lax.broadcasted_iota(jnp.int32, (2, NZ, SLOTS), 2)
    frame = jnp.stack(
        [
            jnp.full((2, 1, 1), -0.5, jnp.float32),
            jnp.array([-1.0, 0.0], jnp.float32).reshape(2, 1, 1),
            jnp.full((2, 1, 1), -0.5, jnp.float32),
        ]
    )
    side = jnp.where(lax.axis_index("gx") % 2 == 0, 1.0, -1.0)

    def forces_of(own):
        near, far = exchange_x(own)
        square, inner_bf, own_bf = density_part(own, own, INNER)
        square, far, near = lax.optimization_barrier((square, far, near))
        near, far = near + along(0, side), far - along(0, side)
        received = exchange_y(rows_along_y(own, near, far))
        middle = jnp.concatenate([near, far], axis=1)
        part, middle_bf = density_part(own_bf, middle, MIDDLE)
        part, received = lax.optimization_barrier((part, received))
        below, above = below_above(received)
        outer = jnp.concatenate([below - along(1, 2.0), above + along(1, 2.0)], axis=1)
        last, outer_bf = density_part(own_bf, outer, OUTER)
        density = DENSITY_SCALE * jnp.maximum(square + part + last - 1.0, 0.0)
        slope = -0.25 * lax.rsqrt(1.0 + density)
        near_slope, far_slope = exchange_x(slope)
        force, turned = force_part(own, own, own_bf, inner_bf, slope, slope, INNER)
        force, far_slope, near_slope = lax.optimization_barrier((force, far_slope, near_slope))
        received = exchange_y(rows_along_y(slope, near_slope, far_slope))
        middle_slope = jnp.concatenate([near_slope, far_slope], axis=0)
        (part,) = force_part(own, middle, own_bf, middle_bf, turned, middle_slope, MIDDLE)
        part, received = lax.optimization_barrier((part, received))
        outer_slope = jnp.concatenate(below_above(received), axis=0)
        (last,) = force_part(own, outer, own_bf, outer_bf, turned, outer_slope, OUTER)
        return force, part, last

    own = jnp.where((places < counts[0][..., None])[None], positions + frame, FAR)
    mark = own[0]
    present = (mark < 0.5 * FAR)[None]
    parts = forces_of(own)
    for step in range(STEPS):
        pushed = jnp.where(present, sum(parts), 0.0)
        if step:
            velocities = velocities + 0.5 * TIME_STEP * pushed
        velocities = velocities + 0.5 * TIME_STEP * pushed
        positions = positions + TIME_STEP * velocities
        parts = forces_of(jnp.where(present, positions + frame, FAR))
    return finish(positions, velocities, mark, parts)


def solution(mesh):
    in_specs = (
        P(None, "gx", "gy", None, None),
        P(None, "gx", "gy", None, None),
        P("gx", "gy", None),
    )
    out_specs = (P(None, "gx", "gy", None, None),) * 3
    return jax.shard_map(shards, mesh=mesh, in_specs=in_specs, out_specs=out_specs, check_vma=False)
```
